256 devices in a mesh: gx: 16 (over z, core), gy: 16 (over y, x).
Axes of the slice: x: 4, y: 4, z: 8, core: 2. Of those that a mesh axis runs over, the one named last changes fastest.
Arguments:
- demand: float32 [16, 1024, 16384], P(None, 'gx', 'gy'), may hold values from -200 to 200, as said below
- initial: float32 [1024, 256], replicated, may hold values from -6 to 6
Outputs:
- factor: float32 [1024, 256], replicated
- core: float32 [256, 16, 16384], P('gx', None, 'gy')
The draws below stay inside these ranges and needn't reach their ends.
Inputs may be any that keep to these rules, and one draw needn't show every extreme that they name: `demand`: Real-valued fluctuations of order one to a few, not all of one scale along x.
All inputs are finite; a program needn't handle non-finite values.
Results may differ from the reference program's by a relative error of at most 0.0003.
Values sent between devices are 32-bit elements; how exact they have to be, the bound alone decides.
No kernel may reach another device: no remote copies, remote signals or barrier semaphores. Data moves between devices by JAX's collectives and lax.ppermute only.
A program may use at most 128 MiB of HBM per device.

```python
import math
import jax
import jax.numpy as jnp
from jax import lax

NX = 1024
NY = 1024
L = 16
R = 256
S = 16
ITERS = 3


def draw_demand(key, part):
    keys = jax.random.split(key, 4)
    noise = jnp.clip(jax.random.normal(keys[0], (L, NX, S * NY), jnp.float32), -6.0, 6.0)
    upper = math.log(3.0)
    scales = jnp.exp(jax.random.uniform(keys[1], (1, NX, 1), jnp.float32, 0.0, upper))
    coefs = 0.7 * jnp.clip(jax.random.normal(keys[2], (4, 1, NX, 1), jnp.float32), -3.0, 3.0)
    factors = jnp.clip(jax.random.normal(keys[3], (4, L, 1, S * NY), jnp.float32), -4.0, 4.0)
    shared = noise
    for index_value in range(4):
        shared = shared + coefs[index_value] * factors[index_value]
    return (scales * shared).astype(jnp.float32)


def centred(stream_key, dims, deviation, reach, dtype=jnp.bfloat16):
    return jnp.clip(deviation * jax.random.normal(stream_key, dims, jnp.float32), -reach, reach).astype(dtype)


def setup_inputs(seed: int = 0) -> dict:
    seeds = jax.random.split(jax.random.key(seed), 3)
    demand = draw_demand(jax.random.fold_in(seeds[2], 71), 0)
    initial = centred(seeds[1], (NX, R), 1.0, 6.0, jnp.float32)
    return {"demand": demand, "initial": initial}


def orthonormal(block):
    weights = jnp.dot(block.T.astype(jnp.float32), block.astype(jnp.float32), precision=lax.Precision.HIGHEST, preferred_element_type=jnp.float32)
    lower_factor = jnp.linalg.cholesky(weights)
    return lax.linalg.triangular_solve(lower_factor, block, left_side=False, lower=True, transpose_a=True)

def reference(demand, initial):

    def add_layer(total, layer):
        return (total + jnp.einsum('xc,zc->xz', layer.astype(jnp.float32), layer.astype(jnp.float32), precision=lax.Precision.HIGHEST, preferred_element_type=jnp.float32), None)
    gram, unused = lax.scan(add_layer, jnp.zeros((NX, NX), jnp.float32), demand)
    gram = gram * (1.0 / (L * S * NY))
    basis = initial
    for iteration in range(ITERS):
        basis = orthonormal(jnp.dot(gram.astype(jnp.float32), basis.astype(jnp.float32), precision=lax.Precision.HIGHEST, preferred_element_type=jnp.float32))

    def project(layer):
        return jnp.einsum('xr,xc->rc', basis.astype(jnp.float32), layer.astype(jnp.float32), precision=lax.Precision.HIGHEST, preferred_element_type=jnp.float32)
    projected = lax.map(project, demand)
    return (basis, jnp.transpose(projected, (1, 0, 2)))
```

```python
import functools

import jax
import jax.numpy as jnp
from jax import lax
from jax.experimental import pallas as pl
from jax.experimental.pallas import tpu as pltpu
from jax.sharding import PartitionSpec as P

L = 16
S = 16
NY = 1024
ITERS = 3
B = 8
T = 128
F32 = jnp.float32
BF16 = jnp.bfloat16
ORDER = (2, 3, 4, 5, 6, 7, 8, 9, 10, 11, 12, 13, 14, 1, 15)
VMEM = pl.BlockSpec(memory_space=pltpu.VMEM)
SMEM = pl.BlockSpec(memory_space=pltpu.SMEM)


def mm(a, b, dims):
    return lax.dot_general(
        a, b, (dims, ((), ())), precision=lax.Precision.HIGHEST, preferred_element_type=F32
    )


def mm16(a, b, dims):
    return lax.dot_general(a, b, (dims, ((), ())), preferred_element_type=F32)


def halves(x):
    high = x.astype(BF16)
    return high, (x - high.astype(F32)).astype(BF16)


def packed_tiles(blocks):
    for p in range(blocks // 2):
        offset = 0
        for i in (p, blocks - 1 - p):
            for j in range(i, blocks):
                yield p, offset, i, j
                offset += 1


def gram_kernel(scale, me_ref, *refs):
    pieces, (hi, lo, out_ref) = refs[:-3], refs[-3:]
    me = me_ref[0]
    rows = pieces[0].shape[0]
    for m, piece in zip((0,) + ORDER, pieces):
        at = pl.ds(pl.multiple_of((me ^ m) * rows, rows), rows)
        hi[at, :], lo[at, :] = halves(piece[...])
    parity = me & 1
    n = hi.shape[0]
    blocks = n // T
    nt = ((1,), (1,))
    for top in range(0, n, 2 * T):
        ah, al = hi[top : top + 2 * T, :], lo[top : top + 2 * T, :]
        bh, bl = hi[top:, :], lo[top:, :]
        product = ((mm16(ah, bl, nt) + mm16(al, bh, nt)) + mm16(ah, bh, nt)) * scale
        for i in (top // T, top // T + 1):
            part = product[i * T - top : (i + 1) * T - top, i * T - top :]
            p = min(i, blocks - 1 - i)
            offset = 0 if i == p else (blocks - p) * T
            out_ref[
                (p // (blocks // 4)) ^ parity,
                p % (blocks // 4) * T : p % (blocks // 4) * T + T,
                offset : offset + part.shape[1],
            ] = part


def gram_packed(pieces, me):
    rows, cols = pieces[0].shape
    n = rows * len(pieces)
    return pl.pallas_call(
        functools.partial(gram_kernel, 1.0 / (L * S * NY)),
        out_shape=(
            jax.ShapeDtypeStruct((n, cols), BF16),
            jax.ShapeDtypeStruct((n, cols), BF16),
            jax.ShapeDtypeStruct((2, n // 4, n + T), F32),
        ),
        in_specs=[SMEM] + [VMEM] * len(pieces),
        out_specs=(VMEM, VMEM, VMEM),
        compiler_params=pltpu.CompilerParams(vmem_limit_bytes=28 << 20),
        name="gram",
    )(me, *pieces)


def inverse_factor(parts):
    groups = T // B
    lane = lax.broadcasted_iota(jnp.int32, (B, T), 1)
    row = lax.broadcasted_iota(jnp.int32, (B, T), 0)
    s = [[ref[i * B : (i + 1) * B, :] for ref in parts] for i in range(groups)]
    for k in range(groups):
        base = k * B
        in_block = (lane >= base) & (lane < base + B)
        rows = [[jnp.broadcast_to(part[j : j + 1, :], (B, T)) for part in s[k]] for j in range(B)]
        a = {
            (j, l): jnp.broadcast_to(rows[j][0][:, base + l : base + l + 1], (B, T))
            for j in range(B)
            for l in range(j, B)
        }
        column = {
            (i, l): jnp.broadcast_to(s[i][0][:, base + l : base + l + 1], (B, T))
            for i in range(k + 1, groups)
            for l in range(B)
        }
        for j in range(B):
            rows[j][0] = jnp.where(in_block, jnp.where(lane == base + j, 1.0, 0.0), rows[j][0])
        for i in range(k + 1, groups):
            s[i][0] = jnp.where(in_block, 0.0, s[i][0])
        done = [jnp.zeros((B, T), F32) for _ in parts]
        for j in range(B):
            root = lax.rsqrt(a[j, j])
            inverse = root * root
            done = [jnp.where(row == j, p * root, d) for p, d in zip(rows[j], done)]
            for i in range(j + 1, B):
                m = a[j, i] * inverse
                for l in range(i, B):
                    a[i, l] = a[i, l] - m * a[j, l]
                rows[i] = [p - m * q for p, q in zip(rows[i], rows[j])]
            for i in range(k + 1, groups):
                m = column[i, j] * inverse
                for l in range(j + 1, B):
                    column[i, l] = column[i, l] - m * a[j, l]
                s[i] = [p - m * q for p, q in zip(s[i], rows[j])]
        done[0] = jnp.where(lane <= row + base, done[0], 0.0)
        for ref, d in zip(parts, done):
            ref[base : base + B, :] = d


def iterate_kernel(iters, me_ref, mine_ref, other_ref, x_ref, hi, lo, q_ref, core_ref, gram, v, w):
    n, r = x_ref.shape
    blocks = n // T
    parity = me_ref[0] & 1
    for p, offset, i, j in packed_tiles(blocks):
        at = (
            slice(p % (blocks // 4) * T, p % (blocks // 4) * T + T),
            slice(offset * T, offset * T + T),
        )
        tile = jnp.where(parity == p // (blocks // 4), mine_ref[at], other_ref[at])
        gram[i * T : (i + 1) * T, j * T : (j + 1) * T] = tile
        if j > i:
            gram[j * T : (j + 1) * T, i * T : (i + 1) * T] = tile.T
    q_ref[...] = x_ref[...]
    tile = 256

    def step(_, carry):
        def product(t, c):
            at = pl.ds(pl.multiple_of(t * tile, tile), tile)
            v[at, :] = mm(gram[at, :], q_ref[...], ((1,), (0,)))
            return c

        lax.fori_loop(0, n // tile, product, 0)
        w[...] = jnp.zeros_like(w)

        def square(t, c):
            at = pl.ds(pl.multiple_of(t * tile, tile), tile)
            block = v[at, :]
            w[...] += mm(block, block, ((0,), (0,)))
            return c

        lax.fori_loop(0, n // tile, square, 0)
        a, b, d = w.at[:T, :T], w.at[:T, T:], w.at[T:, T:]
        inverse_factor([a, b])
        panel = b[...]
        d[...] = d[...] - mm(panel, panel, ((0,), (0,)))
        lower = mm(panel, a[...], ((0,), (0,)))
        inverse_factor([d])
        w[T:, :T] = -mm(d[...], lower, ((1,), (0,)))
        w[:T, T:] = jnp.zeros((T, T), F32)

        def apply(t, c):
            at = pl.ds(pl.multiple_of(t * tile, tile), tile)
            q_ref[at, :] = mm(v[at, :], w[...], ((1,), (1,)))
            return c

        lax.fori_loop(0, n // tile, apply, 0)
        return carry

    lax.fori_loop(0, iters, step, 0)


    qh, ql = halves(q_ref[...])
    tn = ((0,), (0,))

    def project(t, c):
        at = pl.ds(pl.multiple_of(t * tile, tile), tile)
        dh, dl = hi[:, at], lo[:, at]
        core_ref[:, at] = (mm16(qh, dl, tn) + mm16(ql, dh, tn)) + mm16(qh, dh, tn)
        return c

    lax.fori_loop(0, hi.shape[1] // tile, project, 0)


def iterate(mine, other, initial, hi, lo, me):
    n, r = initial.shape
    return pl.pallas_call(
        functools.partial(iterate_kernel, ITERS),
        out_shape=(
            jax.ShapeDtypeStruct((n, r), F32),
            jax.ShapeDtypeStruct((r, hi.shape[1]), F32),
        ),
        in_specs=[SMEM] + [VMEM] * 5,
        out_specs=(VMEM, VMEM),
        scratch_shapes=[
            pltpu.VMEM((n, n), F32),
            pltpu.VMEM((n, r), F32),
            pltpu.VMEM((r, r), F32),
        ],
        compiler_params=pltpu.CompilerParams(vmem_limit_bytes=28 << 20),
        name="iterate",
    )(me, mine, other, initial, hi, lo)


def swap(x, m, size):
    return lax.ppermute(x, "gx", [(i, i ^ m) for i in range(size)])


def on_device(nx, ny, demand, initial):
    here = lax.axis_index("gx")
    me = here.astype(jnp.int32).reshape(1)
    index = here.astype(jnp.uint32)
    pieces = [
        lax.dynamic_slice_in_dim(demand, index ^ jnp.uint32(m), 1, 0)[0] for m in (0,) + ORDER
    ]
    pieces = [pieces[0]] + [swap(p, m, nx) for m, p in zip(ORDER, pieces[1:])]
    hi, lo, packed = gram_packed(pieces, me)
    half = packed[0] + swap(packed[1], 1, nx)
    rows, cols = half.shape
    share = lax.all_to_all(half.reshape(ny, rows // ny, cols), "gy", 0, 0, tiled=True)
    share = jnp.sum(share, 0)
    for m in (8, 4, 2):
        share = share + swap(share, m, nx)
    copies = jnp.broadcast_to(share[None], (ny,) + share.shape)
    half = lax.all_to_all(copies, "gy", 0, 0, tiled=True).reshape(rows, cols)
    basis, part = iterate(half, swap(half, 1, nx), initial, hi, lo, me)
    part = part.reshape(nx, part.shape[0] // nx, part.shape[1])
    core = lax.all_to_all(part, "gx", 0, 0, tiled=True)
    return (basis, jnp.transpose(core, (1, 0, 2)))


def solution(mesh):
    in_specs = (P(None, "gx", "gy"), P())
    out_specs = (P(), P("gx", None, "gy"))
    sizes = (mesh.shape["gx"], mesh.shape["gy"])
    return jax.shard_map(
        functools.partial(on_device, *sizes),
        mesh=mesh,
        in_specs=in_specs,
        out_specs=out_specs,
        check_vma=False,
    )
```

```python
import functools

import jax
import jax.numpy as jnp
from jax import lax
from jax.experimental import pallas as pl
from jax.experimental.pallas import tpu as pltpu
from jax.sharding import PartitionSpec as P

L = 16
S = 16
NY = 1024
ITERS = 3
B = 8
T = 128
F32 = jnp.float32
BF16 = jnp.bfloat16
VMEM = pl.BlockSpec(memory_space=pltpu.VMEM)
SMEM = pl.BlockSpec(memory_space=pltpu.SMEM)


def mm(a, b, dims):
    return lax.dot_general(
        a, b, (dims, ((), ())), precision=lax.Precision.HIGHEST, preferred_element_type=F32
    )


def mm16(a, b, dims):
    return lax.dot_general(a, b, (dims, ((), ())), preferred_element_type=F32)


def halves(x):
    high = x.astype(BF16)
    return high, (x - high.astype(F32)).astype(BF16)


def packed_tiles(blocks):
    for p in range(blocks // 2):
        offset = 0
        for i in (p, blocks - 1 - p):
            for j in range(i, blocks):
                yield p, offset, i, j
                offset += 1


def gram_kernel(scale, me_ref, x_ref, out_ref, hi, lo):
    hi[...], lo[...] = halves(x_ref[...])
    parity = me_ref[0] & 1
    n = hi.shape[0]
    blocks = n // T
    nt = ((1,), (1,))
    for top in range(0, n, 2 * T):
        ah, al = hi[top : top + 2 * T, :], lo[top : top + 2 * T, :]
        bh, bl = hi[top:, :], lo[top:, :]
        product = ((mm16(ah, bl, nt) + mm16(al, bh, nt)) + mm16(ah, bh, nt)) * scale
        for i in (top // T, top // T + 1):
            part = product[i * T - top : (i + 1) * T - top, i * T - top :]
            p = min(i, blocks - 1 - i)
            offset = 0 if i == p else (blocks - p) * T
            out_ref[
                (p // (blocks // 4)) ^ parity,
                p % (blocks // 4) * T : p % (blocks // 4) * T + T,
                offset : offset + part.shape[1],
            ] = part


def gram_packed(x, me):
    n, cols = x.shape
    return pl.pallas_call(
        functools.partial(gram_kernel, 1.0 / (L * S * NY)),
        out_shape=jax.ShapeDtypeStruct((2, n // 4, n + T), F32),
        in_specs=[SMEM, VMEM],
        out_specs=VMEM,
        scratch_shapes=[pltpu.VMEM((n, cols), BF16), pltpu.VMEM((n, cols), BF16)],
        compiler_params=pltpu.CompilerParams(vmem_limit_bytes=28 << 20),
        name="gram",
    )(me, x)


def inverse_factor(parts):
    groups = T // B
    lane = lax.broadcasted_iota(jnp.int32, (B, T), 1)
    row = lax.broadcasted_iota(jnp.int32, (B, T), 0)
    s = [[ref[i * B : (i + 1) * B, :] for ref in parts] for i in range(groups)]
    for k in range(groups):
        base = k * B
        in_block = (lane >= base) & (lane < base + B)
        rows = [[jnp.broadcast_to(part[j : j + 1, :], (B, T)) for part in s[k]] for j in range(B)]
        a = {
            (j, l): jnp.broadcast_to(rows[j][0][:, base + l : base + l + 1], (B, T))
            for j in range(B)
            for l in range(j, B)
        }
        column = {
            (i, l): jnp.broadcast_to(s[i][0][:, base + l : base + l + 1], (B, T))
            for i in range(k + 1, groups)
            for l in range(B)
        }
        for j in range(B):
            rows[j][0] = jnp.where(in_block, jnp.where(lane == base + j, 1.0, 0.0), rows[j][0])
        for i in range(k + 1, groups):
            s[i][0] = jnp.where(in_block, 0.0, s[i][0])
        done = [jnp.zeros((B, T), F32) for _ in parts]
        for j in range(B):
            root = lax.rsqrt(a[j, j])
            inverse = root * root
            done = [jnp.where(row == j, p * root, d) for p, d in zip(rows[j], done)]
            for i in range(j + 1, B):
                m = a[j, i] * inverse
                for l in range(i, B):
                    a[i, l] = a[i, l] - m * a[j, l]
                rows[i] = [p - m * q for p, q in zip(rows[i], rows[j])]
            for i in range(k + 1, groups):
                m = column[i, j] * inverse
                for l in range(j + 1, B):
                    column[i, l] = column[i, l] - m * a[j, l]
                s[i] = [p - m * q for p, q in zip(s[i], rows[j])]
        done[0] = jnp.where(lane <= row + base, done[0], 0.0)
        for ref, d in zip(parts, done):
            ref[base : base + B, :] = d


def iterate_kernel(iters, me_ref, mine_ref, other_ref, x_ref, d_ref, q_ref, core_ref, gram, v, w):
    n, r = x_ref.shape
    blocks = n // T
    parity = me_ref[0] & 1
    for p, offset, i, j in packed_tiles(blocks):
        at = (
            slice(p % (blocks // 4) * T, p % (blocks // 4) * T + T),
            slice(offset * T, offset * T + T),
        )
        tile = jnp.where(parity == p // (blocks // 4), mine_ref[at], other_ref[at])
        gram[i * T : (i + 1) * T, j * T : (j + 1) * T] = tile
        if j > i:
            gram[j * T : (j + 1) * T, i * T : (i + 1) * T] = tile.T
    q_ref[...] = x_ref[...]
    tile = 256

    def step(_, carry):
        w[...] = jnp.zeros_like(w)

        def product(t, c):
            at = pl.ds(pl.multiple_of(t * tile, tile), tile)
            block = mm(gram[at, :], q_ref[...], ((1,), (0,)))
            v[at, :] = block
            w[...] += mm(block, block, ((0,), (0,)))
            return c

        lax.fori_loop(0, n // tile, product, 0)
        a, b, d = w.at[:T, :T], w.at[:T, T:], w.at[T:, T:]
        inverse_factor([a, b])
        panel = b[...]
        d[...] = d[...] - mm(panel, panel, ((0,), (0,)))
        lower = mm(panel, a[...], ((0,), (0,)))
        inverse_factor([d])
        w[T:, :T] = -mm(d[...], lower, ((1,), (0,)))
        w[:T, T:] = jnp.zeros((T, T), F32)

        def apply(t, c):
            at = pl.ds(pl.multiple_of(t * tile, tile), tile)
            q_ref[at, :] = mm(v[at, :], w[...], ((1,), (1,)))
            return c

        lax.fori_loop(0, n // tile, apply, 0)
        return carry

    lax.fori_loop(0, iters, step, 0)


    qh, ql = halves(q_ref[...])
    tn = ((0,), (0,))

    def project(t, c):
        at = pl.ds(pl.multiple_of(t * tile, tile), tile)
        dh, dl = halves(d_ref[:, at])
        core_ref[:, at] = (mm16(qh, dl, tn) + mm16(ql, dh, tn)) + mm16(qh, dh, tn)
        return c

    lax.fori_loop(0, d_ref.shape[1] // tile, project, 0)


def iterate(mine, other, initial, demand, me):
    n, r = initial.shape
    return pl.pallas_call(
        functools.partial(iterate_kernel, ITERS),
        out_shape=(
            jax.ShapeDtypeStruct((n, r), F32),
            jax.ShapeDtypeStruct((r, demand.shape[1]), F32),
        ),
        in_specs=[SMEM] + [VMEM] * 4,
        out_specs=(VMEM, VMEM),
        scratch_shapes=[
            pltpu.VMEM((n, n), F32),
            pltpu.VMEM((n, r), F32),
            pltpu.VMEM((r, r), F32),
        ],
        compiler_params=pltpu.CompilerParams(vmem_limit_bytes=28 << 20),
        name="iterate",
    )(me, mine, other, initial, demand)


def swap(x, m, size):
    return lax.ppermute(x, "gx", [(i, i ^ m) for i in range(size)])


def on_device(nx, ny, demand, initial):
    me = lax.axis_index("gx").astype(jnp.int32).reshape(1)
    fibres = lax.all_to_all(demand, "gx", 0, 1, tiled=True)[0]
    packed = gram_packed(fibres, me)
    half = packed[0] + swap(packed[1], 1, nx)
    rows, cols = half.shape
    share = lax.all_to_all(half.reshape(ny, rows // ny, cols), "gy", 0, 0, tiled=True)
    share = jnp.sum(share, 0)
    chips = nx // 2
    columns = [list(range(core, nx, 2)) for core in (0, 1)]
    part = share.reshape(chips, share.shape[0] // chips, cols)
    part = lax.all_to_all(part, "gx", 0, 0, tiled=True, axis_index_groups=columns)
    part = jnp.broadcast_to(jnp.sum(part, 0)[None], part.shape)
    part = lax.all_to_all(part, "gx", 0, 0, tiled=True, axis_index_groups=columns)
    share = part.reshape(share.shape)
    copies = jnp.broadcast_to(share[None], (ny,) + share.shape)
    half = lax.all_to_all(copies, "gy", 0, 0, tiled=True).reshape(rows, cols)
    basis, part = iterate(half, swap(half, 1, nx), initial, fibres, me)
    part = part.reshape(nx, part.shape[0] // nx, part.shape[1])
    core = lax.all_to_all(part, "gx", 0, 0, tiled=True)
    return (basis, jnp.transpose(core, (1, 0, 2)))


def solution(mesh):
    in_specs = (P(None, "gx", "gy"), P())
    out_specs = (P(), P("gx", None, "gy"))
    sizes = (mesh.shape["gx"], mesh.shape["gy"])
    return jax.shard_map(
        functools.partial(on_device, *sizes),
        mesh=mesh,
        in_specs=in_specs,
        out_specs=out_specs,
        check_vma=False,
    )
```

```python
import functools

import jax
import jax.numpy as jnp
from jax import lax
from jax.experimental import pallas as pl
from jax.experimental.pallas import tpu as pltpu
from jax.sharding import PartitionSpec as P

L = 16
S = 16
NY = 1024
ITERS = 3
B = 8
SUP = 2
TILE = 512
T = 128
F32 = jnp.float32
BF16 = jnp.bfloat16
VMEM = pl.BlockSpec(memory_space=pltpu.VMEM)
SMEM = pl.BlockSpec(memory_space=pltpu.SMEM)


def mm(a, b, dims):
    return lax.dot_general(
        a, b, (dims, ((), ())), precision=lax.Precision.HIGHEST, preferred_element_type=F32
    )


def mm16(a, b, dims):
    return lax.dot_general(a, b, (dims, ((), ())), preferred_element_type=F32)


def halves(x):
    high = x.astype(BF16)
    return high, (x - high.astype(F32)).astype(BF16)


def packed_tiles(blocks):
    for p in range(blocks // 2):
        offset = 0
        for i in (p, blocks - 1 - p):
            for j in range(i, blocks):
                yield p, offset, i, j
                offset += 1


def gram_kernel(scale, me_ref, x_hbm, out_ref, x_ref, hi, lo, sems):
    parity = me_ref[0] & 1
    n = hi.shape[0]
    blocks = n // T
    nt = ((1,), (1,))
    tops = list(reversed(range(0, n, 2 * T)))
    copies = []
    for c, top in enumerate(tops):
        at = pl.ds(top, 2 * T)
        copies.append(pltpu.make_async_copy(x_hbm.at[at, :], x_ref.at[at, :], sems.at[c]))
        copies[-1].start()
    for copy, top in zip(copies, tops):
        copy.wait()
        hi[top : top + 2 * T, :], lo[top : top + 2 * T, :] = halves(x_ref[top : top + 2 * T, :])
        ah, al = hi[top : top + 2 * T, :], lo[top : top + 2 * T, :]
        bh, bl = hi[top:, :], lo[top:, :]
        mixed, main = mm16(ah, bl, nt), mm16(ah, bh, nt)
        own = mixed[:, : 2 * T]
        product = [((own + own.T) + main[:, : 2 * T]) * scale]
        if top + 2 * T < n:
            other = mm16(al, bh[2 * T :, :], nt)
            product.append(((mixed[:, 2 * T :] + other) + main[:, 2 * T :]) * scale)
        product = jnp.concatenate(product, 1)
        for i in (top // T, top // T + 1):
            part = product[i * T - top : (i + 1) * T - top, i * T - top :]
            p = min(i, blocks - 1 - i)
            offset = 0 if i == p else (blocks - p) * T
            out_ref[
                (p // (blocks // 4)) ^ parity,
                p % (blocks // 4) * T : p % (blocks // 4) * T + T,
                offset : offset + part.shape[1],
            ] = part


def gram_packed(x, me):
    n, cols = x.shape
    return pl.pallas_call(
        functools.partial(gram_kernel, 1.0 / (L * S * NY)),
        out_shape=jax.ShapeDtypeStruct((2, n // 4, n + T), F32),
        in_specs=[SMEM, pl.BlockSpec(memory_space=pl.ANY)],
        out_specs=VMEM,
        scratch_shapes=[
            pltpu.VMEM((n, cols), F32),
            pltpu.VMEM((n, cols), BF16),
            pltpu.VMEM((n, cols), BF16),
            pltpu.SemaphoreType.DMA((n // (2 * T),)),
        ],
        compiler_params=pltpu.CompilerParams(vmem_limit_bytes=28 << 20),
        name="gram",
    )(me, x)


def thirds(x):
    high = x.astype(BF16).astype(F32)
    rest = x - high
    middle = rest.astype(BF16).astype(F32)
    return high, middle, rest - middle


def spread(x, j):
    return jnp.broadcast_to(x[j : j + 1, :], x.shape)


def inverse_factor(parts):
    groups = T // B
    lane = lax.broadcasted_iota(jnp.int32, (B, T), 1)
    row = lax.broadcasted_iota(jnp.int32, (B, T), 0)
    s = [[ref[i * B : (i + 1) * B, :] for ref in parts] for i in range(groups)]
    held = []
    for k in range(groups):
        base = k * B
        in_block = (lane >= base) & (lane < base + B)
        column = {
            (i, l): jnp.broadcast_to(s[i][0][:, base + l : base + l + 1], (B, T))
            for i in range(k, min((k // SUP + 2) * SUP, groups))
            for l in range(B)
        }
        s[k][0] = jnp.where(in_block, jnp.where(lane == row + base, 1.0, 0.0), s[k][0])
        near = min((k // SUP + 2) * SUP, groups)
        for i in range(k + 1, groups):
            s[i][0] = jnp.where(in_block, 0.0, s[i][0])
        scale = jnp.zeros((B, T), F32)
        for j in range(B):
            root = lax.rsqrt(spread(column[k, j], j))
            inverse = root * root
            scale = jnp.where(row == j, root, scale)
            across = {l: spread(column[k, l], j) for l in range(j + 1, B)}
            lead = [spread(part, j) for part in s[k]]
            for i in range(k, near):
                m = column[i, j] * inverse
                if i == k:
                    m = jnp.where(row > j, m, 0.0)
                for l in range(j + 1, B):
                    column[i, l] = column[i, l] - m * across[l]
                s[i] = [p - m * q for p, q in zip(s[i], lead)]
        done = [p * scale for p in s[k]]
        later = (lane >= base + B) & (lane < (k // SUP + 1) * SUP * B)
        held.append([jnp.where(later, 0.0, done[0])] + done[1:])
        if k % SUP == SUP - 1:
            if near < groups:
                left = thirds(jnp.concatenate([h[0] for h in held], 0))
                right = thirds(jnp.concatenate([jnp.concatenate(h, 1) for h in held], 0))
                left = jnp.concatenate([left[c] for c in (0, 0, 1, 1, 0, 2)], 0).astype(BF16)
                right = jnp.concatenate([right[c] for c in (0, 1, 0, 1, 2, 0)], 0).astype(BF16)
                far = mm16(left, right, ((0,), (0,)))
                for i in range(near, groups):
                    s[i] = [
                        p - far[i * B : (i + 1) * B, c * T : (c + 1) * T]
                        for c, p in enumerate(s[i])
                    ]
            held = []
        done = list(done)
        done[0] = jnp.where(lane <= row + base, done[0], 0.0)
        for ref, d in zip(parts, done):
            ref[base : base + B, :] = d


def iterate_kernel(
    iters, me_ref, mine_ref, other_ref, x_ref, d_hbm, q_ref, core_ref, gram, split, v, w, cross,
    d_ref, sem,
):
    fetch = pltpu.make_async_copy(d_hbm, d_ref, sem)
    fetch.start()
    n, r = x_ref.shape
    blocks = n // T
    parity = me_ref[0] & 1
    for p, offset, i, j in packed_tiles(blocks):
        at = (
            slice(p % (blocks // 4) * T, p % (blocks // 4) * T + T),
            slice(offset * T, offset * T + T),
        )
        tile = jnp.where(parity == p // (blocks // 4), mine_ref[at], other_ref[at])
        for c, third in enumerate(thirds(tile)):
            gram[c, i * T : (i + 1) * T, j * T : (j + 1) * T] = third.astype(BF16)
            if j > i:
                gram[c, j * T : (j + 1) * T, i * T : (i + 1) * T] = third.T.astype(BF16)
    q_ref[...] = x_ref[...]

    def step(_, carry):
        for c, third in enumerate(thirds(q_ref[...])):
            split[c] = third.astype(BF16)

        def product(t, carry):
            at = pl.ds(pl.multiple_of(t * TILE, TILE), TILE)

            def term(i, j):
                return mm16(gram[i, at, :], split[j], ((1,), (0,)))

            block = (
                ((term(0, 2) + term(1, 1)) + term(2, 0)) + (term(0, 1) + term(1, 0))
            ) + term(0, 0)
            for c, third in enumerate(thirds(block)):
                v[c, at, :] = third.astype(BF16)
            return carry

        lax.fori_loop(0, n // TILE, product, 0)
        w[...] = jnp.zeros_like(w)
        cross[...] = jnp.zeros_like(cross)

        def square(t, carry):
            at = pl.ds(pl.multiple_of(t * TILE, TILE), TILE)
            high, middle, low = v[0, at, :], v[1, at, :], v[2, at, :]
            tn = ((0,), (0,))
            w[...] += mm16(middle, middle, tn) + mm16(high, high, tn)
            cross[...] += mm16(high, low, tn) + mm16(high, middle, tn)
            return carry

        lax.fori_loop(0, n // TILE, square, 0)
        w[...] += cross[...] + cross[...].T
        a, b, d = w.at[:T, :T], w.at[:T, T:], w.at[T:, T:]
        inverse_factor([a, b])
        panel = b[...]
        d[...] = d[...] - mm(panel, panel, ((0,), (0,)))
        lower = mm(panel, a[...], ((0,), (0,)))
        inverse_factor([d])
        w[T:, :T] = -mm(d[...], lower, ((1,), (0,)))
        w[:T, T:] = jnp.zeros((T, T), F32)

        inverse = [third.astype(BF16) for third in thirds(w[...])]

        def apply(t, carry):
            at = pl.ds(pl.multiple_of(t * TILE, TILE), TILE)

            def term(i, j):
                return mm16(v[i, at, :], inverse[j], ((1,), (1,)))

            q_ref[at, :] = (
                ((term(0, 2) + term(1, 1)) + term(2, 0)) + (term(0, 1) + term(1, 0))
            ) + term(0, 0)
            return carry

        lax.fori_loop(0, n // TILE, apply, 0)
        return carry

    lax.fori_loop(0, iters, step, 0)
    fetch.wait()
    qh, ql = halves(q_ref[...])
    tn = ((0,), (0,))

    def project(t, c):
        at = pl.ds(pl.multiple_of(t * TILE, TILE), TILE)
        dh, dl = halves(d_ref[:, at])
        core_ref[:, at] = (mm16(qh, dl, tn) + mm16(ql, dh, tn)) + mm16(qh, dh, tn)
        return c

    lax.fori_loop(0, d_ref.shape[1] // TILE, project, 0)


def iterate(mine, other, initial, demand, me):
    n, r = initial.shape
    return pl.pallas_call(
        functools.partial(iterate_kernel, ITERS),
        out_shape=(
            jax.ShapeDtypeStruct((n, r), F32),
            jax.ShapeDtypeStruct((r, demand.shape[1]), F32),
        ),
        in_specs=[SMEM, VMEM, VMEM, VMEM, pl.BlockSpec(memory_space=pl.ANY)],
        out_specs=(VMEM, VMEM),
        scratch_shapes=[
            pltpu.VMEM((3, n, n), BF16),
            pltpu.VMEM((3, n, r), BF16),
            pltpu.VMEM((3, n, r), BF16),
            pltpu.VMEM((r, r), F32),
            pltpu.VMEM((r, r), F32),
            pltpu.VMEM(demand.shape, F32),
            pltpu.SemaphoreType.DMA,
        ],
        compiler_params=pltpu.CompilerParams(vmem_limit_bytes=28 << 20),
        name="iterate",
    )(me, mine, other, initial, demand)


def swap(x, m, size):
    return lax.ppermute(x, "gx", [(i, i ^ m) for i in range(size)])


def on_device(nx, ny, demand, initial):
    me = lax.axis_index("gx").astype(jnp.int32).reshape(1)
    fibres = lax.all_to_all(demand, "gx", 0, 1, tiled=True)[0]
    packed = gram_packed(fibres, me)
    half = packed[0] + swap(packed[1], 1, nx)
    rows, cols = half.shape
    share = lax.all_to_all(half.reshape(ny, rows // ny, cols), "gy", 0, 0, tiled=True)
    share = jnp.sum(share, 0)
    for m in (2, 4, 8):
        share = share + swap(share, m, nx)
    copies = jnp.broadcast_to(share[None], (ny,) + share.shape)
    half = lax.all_to_all(copies, "gy", 0, 0, tiled=True).reshape(rows, cols)
    basis, part = iterate(half, swap(half, 1, nx), initial, fibres, me)
    part = part.reshape(nx, part.shape[0] // nx, part.shape[1])
    core = lax.all_to_all(part, "gx", 0, 0, tiled=True)
    return (basis, jnp.transpose(core, (1, 0, 2)))


def solution(mesh):
    in_specs = (P(None, "gx", "gy"), P())
    out_specs = (P(), P("gx", None, "gy"))
    sizes = (mesh.shape["gx"], mesh.shape["gy"])
    return jax.shard_map(
        functools.partial(on_device, *sizes),
        mesh=mesh,
        in_specs=in_specs,
        out_specs=out_specs,
        check_vma=False,
    )
```

```python
import functools

import jax
import jax.numpy as jnp
from jax import lax
from jax.experimental import pallas as pl
from jax.experimental.pallas import tpu as pltpu
from jax.sharding import PartitionSpec as P

L = 16
S = 16
NY = 1024
ITERS = 3
B = 8
SUP = 2
TILE = 512
T = 128
F32 = jnp.float32
BF16 = jnp.bfloat16
VMEM = pl.BlockSpec(memory_space=pltpu.VMEM)
SMEM = pl.BlockSpec(memory_space=pltpu.SMEM)


def mm(a, b, dims):
    return lax.dot_general(
        a, b, (dims, ((), ())), precision=lax.Precision.HIGHEST, preferred_element_type=F32
    )


def mm16(a, b, dims):
    return lax.dot_general(a, b, (dims, ((), ())), preferred_element_type=F32)


def halves(x):
    high = x.astype(BF16)
    return high, (x - high.astype(F32)).astype(BF16)


def packed_tiles(blocks):
    for p in range(blocks // 2):
        offset = 0
        for i in (p, blocks - 1 - p):
            for j in range(i, blocks):
                yield p, offset, i, j
                offset += 1


def gram_kernel(scale, flip, me_ref, x_hbm, out_ref, x_ref, hi, lo, sems):
    n = hi.shape[0]
    blocks = n // T
    nt = ((1,), (1,))
    half = (me_ref[0] & 1) ^ flip

    def rows_from(tops):
        waiting = []
        for c, top in enumerate(reversed(range(min(tops), n, 2 * T))):
            at = pl.ds(top, 2 * T)
            copy = pltpu.make_async_copy(x_hbm.at[at, :], x_ref.at[at, :], sems.at[c])
            copy.start()
            waiting.append((top, copy))
        for top in tops:
            while waiting and waiting[0][0] >= top:
                ready, copy = waiting.pop(0)
                copy.wait()
                at = slice(ready, ready + 2 * T)
                hi[at, :], lo[at, :] = halves(x_ref[at, :])
            ah, al = hi[top : top + 2 * T, :], lo[top : top + 2 * T, :]
            bh, bl = hi[top:, :], lo[top:, :]
            mixed, main = mm16(ah, bl, nt), mm16(ah, bh, nt)
            own = mixed[:, : 2 * T]
            product = [((own + own.T) + main[:, : 2 * T]) * scale]
            if top + 2 * T < n:
                other = mm16(al, bh[2 * T :, :], nt)
                product.append(((mixed[:, 2 * T :] + other) + main[:, 2 * T :]) * scale)
            product = jnp.concatenate(product, 1)
            for i in (top // T, top // T + 1):
                part = product[i * T - top : (i + 1) * T - top, i * T - top :]
                p = min(i, blocks - 1 - i)
                offset = 0 if i == p else (blocks - p) * T
                row = p % (blocks // 4) * T
                out_ref[row : row + T, offset : offset + part.shape[1]] = part

    @pl.when(half == 0)
    def _():
        rows_from((n - 2 * T, 0))

    @pl.when(half == 1)
    def _():
        rows_from((n - 4 * T, 2 * T))


def gram_half(x, me, flip):
    n, cols = x.shape
    return pl.pallas_call(
        functools.partial(gram_kernel, 1.0 / (L * S * NY), flip),
        out_shape=jax.ShapeDtypeStruct((n // 4, n + T), F32),
        in_specs=[SMEM, pl.BlockSpec(memory_space=pl.ANY)],
        out_specs=VMEM,
        scratch_shapes=[
            pltpu.VMEM((n, cols), F32),
            pltpu.VMEM((n, cols), BF16),
            pltpu.VMEM((n, cols), BF16),
            pltpu.SemaphoreType.DMA((n // (2 * T),)),
        ],
        compiler_params=pltpu.CompilerParams(vmem_limit_bytes=28 << 20),
        cost_estimate=pl.CostEstimate(
            flops=2 * n * n * cols, bytes_accessed=5 * n * cols, transcendentals=0
        ),
        name="gram",
    )(me, x)


def thirds(x):
    high = x.astype(BF16).astype(F32)
    rest = x - high
    middle = rest.astype(BF16).astype(F32)
    return high, middle, rest - middle


def spread(x, j):
    return jnp.broadcast_to(x[j : j + 1, :], x.shape)


def inverse_factor(parts):
    groups = T // B
    lane = lax.broadcasted_iota(jnp.int32, (B, T), 1)
    row = lax.broadcasted_iota(jnp.int32, (B, T), 0)
    s = [[ref[i * B : (i + 1) * B, :] for ref in parts] for i in range(groups)]
    held = []
    for k in range(groups):
        base = k * B
        in_block = (lane >= base) & (lane < base + B)
        column = {
            (i, l): jnp.broadcast_to(s[i][0][:, base + l : base + l + 1], (B, T))
            for i in range(k, min((k // SUP + 2) * SUP, groups))
            for l in range(B)
        }
        s[k][0] = jnp.where(in_block, jnp.where(lane == row + base, 1.0, 0.0), s[k][0])
        near = min((k // SUP + 2) * SUP, groups)
        for i in range(k + 1, groups):
            s[i][0] = jnp.where(in_block, 0.0, s[i][0])
        scale = jnp.zeros((B, T), F32)
        for j in range(B):
            root = lax.rsqrt(spread(column[k, j], j))
            inverse = root * root
            scale = jnp.where(row == j, root, scale)
            across = {l: spread(column[k, l], j) for l in range(j + 1, B)}
            lead = [spread(part, j) for part in s[k]]
            for i in range(k, near):
                m = column[i, j] * inverse
                if i == k:
                    m = jnp.where(row > j, m, 0.0)
                for l in range(j + 1, B):
                    column[i, l] = column[i, l] - m * across[l]
                s[i] = [p - m * q for p, q in zip(s[i], lead)]
        done = [p * scale for p in s[k]]
        later = (lane >= base + B) & (lane < (k // SUP + 1) * SUP * B)
        held.append([jnp.where(later, 0.0, done[0])] + done[1:])
        if k % SUP == SUP - 1:
            if near < groups:
                left = thirds(jnp.concatenate([h[0] for h in held], 0))
                right = thirds(jnp.concatenate([jnp.concatenate(h, 1) for h in held], 0))
                left = jnp.concatenate([left[c] for c in (0, 0, 1, 1, 0, 2)], 0).astype(BF16)
                right = jnp.concatenate([right[c] for c in (0, 1, 0, 1, 2, 0)], 0).astype(BF16)
                far = mm16(left, right, ((0,), (0,)))
                for i in range(near, groups):
                    s[i] = [
                        p - far[i * B : (i + 1) * B, c * T : (c + 1) * T]
                        for c, p in enumerate(s[i])
                    ]
            held = []
        done = list(done)
        done[0] = jnp.where(lane <= row + base, done[0], 0.0)
        for ref, d in zip(parts, done):
            ref[base : base + B, :] = d


def iterate_kernel(
    iters, me_ref, mine_ref, other_ref, x_ref, d_hbm, q_ref, core_ref, gram, split, v, w, cross,
    d_ref, sem,
):
    fetch = pltpu.make_async_copy(d_hbm, d_ref, sem)
    fetch.start()
    n, r = x_ref.shape
    blocks = n // T
    parity = me_ref[0] & 1
    for p, offset, i, j in packed_tiles(blocks):
        at = (
            slice(p % (blocks // 4) * T, p % (blocks // 4) * T + T),
            slice(offset * T, offset * T + T),
        )
        tile = jnp.where(parity == p // (blocks // 4), mine_ref[at], other_ref[at])
        for c, third in enumerate(thirds(tile)):
            third = third.astype(BF16)
            gram[c, i * T : (i + 1) * T, j * T : (j + 1) * T] = third
            if j > i:
                gram[c, j * T : (j + 1) * T, i * T : (i + 1) * T] = third.T
    q_ref[...] = x_ref[...]

    def step(_, carry):
        for c, third in enumerate(thirds(q_ref[...])):
            split[c] = third.astype(BF16)

        def product(t, carry):
            at = pl.ds(pl.multiple_of(t * TILE, TILE), TILE)

            def term(i, j):
                return mm16(gram[i, at, :], split[j], ((1,), (0,)))

            block = (
                ((term(0, 2) + term(1, 1)) + term(2, 0)) + (term(0, 1) + term(1, 0))
            ) + term(0, 0)
            for c, third in enumerate(thirds(block)):
                v[c, at, :] = third.astype(BF16)
            return carry

        lax.fori_loop(0, n // TILE, product, 0)
        w[...] = jnp.zeros_like(w)
        cross[...] = jnp.zeros_like(cross)

        def square(t, carry):
            at = pl.ds(pl.multiple_of(t * TILE, TILE), TILE)
            high, middle, low = v[0, at, :], v[1, at, :], v[2, at, :]
            tn = ((0,), (0,))
            w[...] += mm16(middle, middle, tn) + mm16(high, high, tn)
            cross[...] += mm16(high, low, tn) + mm16(high, middle, tn)
            return carry

        lax.fori_loop(0, n // TILE, square, 0)
        w[...] += cross[...] + cross[...].T
        a, b, d = w.at[:T, :T], w.at[:T, T:], w.at[T:, T:]
        inverse_factor([a, b])
        panel = b[...]
        d[...] = d[...] - mm(panel, panel, ((0,), (0,)))
        lower = mm(panel, a[...], ((0,), (0,)))
        inverse_factor([d])
        w[T:, :T] = -mm(d[...], lower, ((1,), (0,)))
        w[:T, T:] = jnp.zeros((T, T), F32)

        inverse = [third.astype(BF16) for third in thirds(w[...])]

        def apply(t, carry):
            at = pl.ds(pl.multiple_of(t * TILE, TILE), TILE)

            def term(i, j):
                return mm16(v[i, at, :], inverse[j], ((1,), (1,)))

            q_ref[at, :] = (
                ((term(0, 2) + term(1, 1)) + term(2, 0)) + (term(0, 1) + term(1, 0))
            ) + term(0, 0)
            return carry

        lax.fori_loop(0, n // TILE, apply, 0)
        return carry

    lax.fori_loop(0, iters, step, 0)
    fetch.wait()
    qh, ql = halves(q_ref[...])
    tn = ((0,), (0,))

    def project(t, c):
        at = pl.ds(pl.multiple_of(t * TILE, TILE), TILE)
        dh, dl = halves(d_ref[:, at])
        core_ref[:, at] = (mm16(qh, dl, tn) + mm16(ql, dh, tn)) + mm16(qh, dh, tn)
        return c

    lax.fori_loop(0, d_ref.shape[1] // TILE, project, 0)


def iterate(mine, other, initial, demand, me):
    n, r = initial.shape
    return pl.pallas_call(
        functools.partial(iterate_kernel, ITERS),
        out_shape=(
            jax.ShapeDtypeStruct((n, r), F32),
            jax.ShapeDtypeStruct((r, demand.shape[1]), F32),
        ),
        in_specs=[SMEM, VMEM, VMEM, VMEM, pl.BlockSpec(memory_space=pl.ANY)],
        out_specs=(VMEM, VMEM),
        scratch_shapes=[
            pltpu.VMEM((3, n, n), BF16),
            pltpu.VMEM((3, n, r), BF16),
            pltpu.VMEM((3, n, r), BF16),
            pltpu.VMEM((r, r), F32),
            pltpu.VMEM((r, r), F32),
            pltpu.VMEM(demand.shape, F32),
            pltpu.SemaphoreType.DMA,
        ],
        compiler_params=pltpu.CompilerParams(vmem_limit_bytes=28 << 20),
        name="iterate",
    )(me, mine, other, initial, demand)


def swap(x, m, size):
    return lax.ppermute(x, "gx", [(i, i ^ m) for i in range(size)])


def on_device(nx, ny, demand, initial):
    me = lax.axis_index("gx").astype(jnp.int32).reshape(1)
    fibres = lax.all_to_all(demand, "gx", 0, 1, tiled=True)[0]
    theirs = swap(gram_half(fibres, me, 1), 1, nx)
    half = gram_half(fibres, me, 0) + theirs
    rows, cols = half.shape
    share = lax.all_to_all(half.reshape(ny, rows // ny, cols), "gy", 0, 0, tiled=True)
    share = jnp.sum(share, 0)
    for m in (2, 4, 8):
        share = share + swap(share, m, nx)
    copies = jnp.broadcast_to(share[None], (ny,) + share.shape)
    half = lax.all_to_all(copies, "gy", 0, 0, tiled=True).reshape(rows, cols)
    basis, part = iterate(half, swap(half, 1, nx), initial, fibres, me)
    part = part.reshape(nx, part.shape[0] // nx, part.shape[1])
    core = lax.all_to_all(part, "gx", 0, 0, tiled=True)
    return (basis, jnp.transpose(core, (1, 0, 2)))


def solution(mesh):
    in_specs = (P(None, "gx", "gy"), P())
    out_specs = (P(), P("gx", None, "gy"))
    sizes = (mesh.shape["gx"], mesh.shape["gy"])
    return jax.shard_map(
        functools.partial(on_device, *sizes),
        mesh=mesh,
        in_specs=in_specs,
        out_specs=out_specs,
        check_vma=False,
    )
```

```python
import functools

import jax
import jax.numpy as jnp
from jax import lax
from jax.experimental import pallas as pl
from jax.experimental.pallas import tpu as pltpu
from jax.sharding import PartitionSpec as P

L = 16
S = 16
NY = 1024
ITERS = 3
B = 8
SUP = 2
TILE = 512
T = 128
F32 = jnp.float32
BF16 = jnp.bfloat16
VMEM = pl.BlockSpec(memory_space=pltpu.VMEM)
SMEM = pl.BlockSpec(memory_space=pltpu.SMEM)


def mm(a, b, dims):
    return lax.dot_general(
        a, b, (dims, ((), ())), precision=lax.Precision.HIGHEST, preferred_element_type=F32
    )


def mm16(a, b, dims):
    return lax.dot_general(a, b, (dims, ((), ())), preferred_element_type=F32)


def halves(x):
    high = x.astype(BF16)
    return high, (x - high.astype(F32)).astype(BF16)


def packed_tiles(blocks):
    for p in range(blocks // 2):
        offset = 0
        for i in (p, blocks - 1 - p):
            for j in range(i, blocks):
                yield p, offset, i, j
                offset += 1


def gram_kernel(scale, flip, me_ref, x_hbm, out_ref, x_ref, hi, lo, sems):
    n = hi.shape[0]
    blocks = n // T
    nt = ((1,), (1,))
    half = (me_ref[0] & 1) ^ flip

    def rows_from(tops):
        waiting = []
        for c, top in enumerate(reversed(range(min(tops), n, 2 * T))):
            at = pl.ds(top, 2 * T)
            copy = pltpu.make_async_copy(x_hbm.at[at, :], x_ref.at[at, :], sems.at[c])
            copy.start()
            waiting.append((top, copy))
        for top in tops:
            while waiting and waiting[0][0] >= top:
                ready, copy = waiting.pop(0)
                copy.wait()
                at = slice(ready, ready + 2 * T)
                hi[at, :], lo[at, :] = halves(x_ref[at, :])
            ah, al = hi[top : top + 2 * T, :], lo[top : top + 2 * T, :]
            bh, bl = hi[top:, :], lo[top:, :]
            mixed, main = mm16(ah, bl, nt), mm16(ah, bh, nt)
            own = mixed[:, : 2 * T]
            product = [((own + own.T) + main[:, : 2 * T]) * scale]
            if top + 2 * T < n:
                other = mm16(al, bh[2 * T :, :], nt)
                product.append(((mixed[:, 2 * T :] + other) + main[:, 2 * T :]) * scale)
            product = jnp.concatenate(product, 1)
            for i in (top // T, top // T + 1):
                part = product[i * T - top : (i + 1) * T - top, i * T - top :]
                p = min(i, blocks - 1 - i)
                offset = 0 if i == p else (blocks - p) * T
                row = p % (blocks // 4) * T
                out_ref[row : row + T, offset : offset + part.shape[1]] = part

    @pl.when(half == 0)
    def _():
        rows_from((n - 2 * T, 0))

    @pl.when(half == 1)
    def _():
        rows_from((n - 4 * T, 2 * T))


def gram_half(x, me, flip):
    n, cols = x.shape
    return pl.pallas_call(
        functools.partial(gram_kernel, 1.0 / (L * S * NY), flip),
        out_shape=jax.ShapeDtypeStruct((n // 4, n + T), F32),
        in_specs=[SMEM, pl.BlockSpec(memory_space=pl.ANY)],
        out_specs=VMEM,
        scratch_shapes=[
            pltpu.VMEM((n, cols), F32),
            pltpu.VMEM((n, cols), BF16),
            pltpu.VMEM((n, cols), BF16),
            pltpu.SemaphoreType.DMA((n // (2 * T),)),
        ],
        compiler_params=pltpu.CompilerParams(vmem_limit_bytes=28 << 20),
        cost_estimate=pl.CostEstimate(
            flops=2 * n * n * cols, bytes_accessed=5 * n * cols, transcendentals=0
        ),
        name="gram",
    )(me, x)


def thirds(x):
    high = x.astype(BF16).astype(F32)
    rest = x - high
    middle = rest.astype(BF16).astype(F32)
    return high, middle, rest - middle


def spread(x, j):
    return jnp.broadcast_to(x[j : j + 1, :], x.shape)


def inverse_factor(parts):
    groups = T // B
    lane = lax.broadcasted_iota(jnp.int32, (B, T), 1)
    row = lax.broadcasted_iota(jnp.int32, (B, T), 0)
    s = [[ref[i * B : (i + 1) * B, :] for ref in parts] for i in range(groups)]
    held = []
    for k in range(groups):
        base = k * B
        in_block = (lane >= base) & (lane < base + B)
        column = {
            (i, l): jnp.broadcast_to(s[i][0][:, base + l : base + l + 1], (B, T))
            for i in range(k, min((k // SUP + 2) * SUP, groups))
            for l in range(B)
        }
        s[k][0] = jnp.where(in_block, jnp.where(lane == row + base, 1.0, 0.0), s[k][0])
        near = min((k // SUP + 2) * SUP, groups)
        for i in range(k + 1, groups):
            s[i][0] = jnp.where(in_block, 0.0, s[i][0])
        scale = jnp.zeros((B, T), F32)
        for j in range(B):
            root = lax.rsqrt(spread(column[k, j], j))
            inverse = root * root
            scale = jnp.where(row == j, root, scale)
            across = {l: spread(column[k, l], j) for l in range(j + 1, B)}
            lead = [spread(part, j) for part in s[k]]
            for i in range(k, near):
                m = column[i, j] * inverse
                if i == k:
                    m = jnp.where(row > j, m, 0.0)
                for l in range(j + 1, B):
                    column[i, l] = column[i, l] - m * across[l]
                s[i] = [p - m * q for p, q in zip(s[i], lead)]
        done = [p * scale for p in s[k]]
        later = (lane >= base + B) & (lane < (k // SUP + 1) * SUP * B)
        held.append([jnp.where(later, 0.0, done[0])] + done[1:])
        if k % SUP == SUP - 1:
            if near < groups:
                left = thirds(jnp.concatenate([h[0] for h in held], 0))
                right = thirds(jnp.concatenate([jnp.concatenate(h, 1) for h in held], 0))
                left = jnp.concatenate([left[c] for c in (0, 0, 1, 1, 0, 2)], 0).astype(BF16)
                right = jnp.concatenate([right[c] for c in (0, 1, 0, 1, 2, 0)], 0).astype(BF16)
                far = mm16(left, right, ((0,), (0,)))
                for i in range(near, groups):
                    s[i] = [
                        p - far[i * B : (i + 1) * B, c * T : (c + 1) * T]
                        for c, p in enumerate(s[i])
                    ]
            held = []
        done = list(done)
        done[0] = jnp.where(lane <= row + base, done[0], 0.0)
        for ref, d in zip(parts, done):
            ref[base : base + B, :] = d


def iterate_kernel(
    iters, me_ref, mine_ref, other_ref, x_ref, d_hbm, q_ref, core_ref, gram, split, v, w, cross,
    d_ref, sem,
):
    fetch = pltpu.make_async_copy(d_hbm, d_ref, sem)
    fetch.start()
    n, r = x_ref.shape
    blocks = n // T
    parity = me_ref[0] & 1
    for p, offset, i, j in packed_tiles(blocks):
        at = (
            slice(p % (blocks // 4) * T, p % (blocks // 4) * T + T),
            slice(offset * T, offset * T + T),
        )
        tile = jnp.where(parity == p // (blocks // 4), mine_ref[at], other_ref[at])
        for c, third in enumerate(thirds(tile)):
            third = third.astype(BF16)
            gram[c, i * T : (i + 1) * T, j * T : (j + 1) * T] = third
            if j > i:
                gram[c, j * T : (j + 1) * T, i * T : (i + 1) * T] = third.T
    q_ref[...] = x_ref[...]

    def step(_, carry):
        for c, third in enumerate(thirds(q_ref[...])):
            split[c] = third.astype(BF16)

        def product(t, carry):
            at = pl.ds(pl.multiple_of(t * TILE, TILE), TILE)

            def term(i, j):
                return mm16(gram[i, at, :], split[j], ((1,), (0,)))

            block = (
                ((term(0, 2) + term(1, 1)) + term(2, 0)) + (term(0, 1) + term(1, 0))
            ) + term(0, 0)
            for c, third in enumerate(thirds(block)):
                v[c, at, :] = third.astype(BF16)
            return carry

        lax.fori_loop(0, n // TILE, product, 0, unroll=True)
        w[...] = jnp.zeros_like(w)
        cross[...] = jnp.zeros_like(cross)

        def square(t, carry):
            at = pl.ds(pl.multiple_of(t * TILE, TILE), TILE)
            high, middle, low = v[0, at, :], v[1, at, :], v[2, at, :]
            tn = ((0,), (0,))
            w[...] += mm16(middle, middle, tn) + mm16(high, high, tn)
            cross[...] += mm16(high, low, tn) + mm16(high, middle, tn)
            return carry

        lax.fori_loop(0, n // TILE, square, 0, unroll=True)
        w[...] += cross[...] + cross[...].T
        a, b, d = w.at[:T, :T], w.at[:T, T:], w.at[T:, T:]
        inverse_factor([a, b])
        panel = b[...]
        d[...] = d[...] - mm(panel, panel, ((0,), (0,)))
        lower = mm(panel, a[...], ((0,), (0,)))
        inverse_factor([d])
        w[T:, :T] = -mm(d[...], lower, ((1,), (0,)))
        w[:T, T:] = jnp.zeros((T, T), F32)

        inverse = [third.astype(BF16) for third in thirds(w[...])]

        def apply(t, carry):
            at = pl.ds(pl.multiple_of(t * TILE, TILE), TILE)

            def term(i, j):
                return mm16(v[i, at, :], inverse[j], ((1,), (1,)))

            q_ref[at, :] = (
                ((term(0, 2) + term(1, 1)) + term(2, 0)) + (term(0, 1) + term(1, 0))
            ) + term(0, 0)
            return carry

        lax.fori_loop(0, n // TILE, apply, 0, unroll=True)
        return carry

    lax.fori_loop(0, iters, step, 0)
    fetch.wait()
    qh, ql = halves(q_ref[...])
    tn = ((0,), (0,))

    def project(t, c):
        at = pl.ds(pl.multiple_of(t * TILE, TILE), TILE)
        dh, dl = halves(d_ref[:, at])
        core_ref[:, at] = (mm16(qh, dl, tn) + mm16(ql, dh, tn)) + mm16(qh, dh, tn)
        return c

    lax.fori_loop(0, d_ref.shape[1] // TILE, project, 0, unroll=True)


def iterate(mine, other, initial, demand, me):
    n, r = initial.shape
    return pl.pallas_call(
        functools.partial(iterate_kernel, ITERS),
        out_shape=(
            jax.ShapeDtypeStruct((n, r), F32),
            jax.ShapeDtypeStruct((r, demand.shape[1]), F32),
        ),
        in_specs=[SMEM, VMEM, VMEM, VMEM, pl.BlockSpec(memory_space=pl.ANY)],
        out_specs=(VMEM, VMEM),
        scratch_shapes=[
            pltpu.VMEM((3, n, n), BF16),
            pltpu.VMEM((3, n, r), BF16),
            pltpu.VMEM((3, n, r), BF16),
            pltpu.VMEM((r, r), F32),
            pltpu.VMEM((r, r), F32),
            pltpu.VMEM(demand.shape, F32),
            pltpu.SemaphoreType.DMA,
        ],
        compiler_params=pltpu.CompilerParams(vmem_limit_bytes=28 << 20),
        name="iterate",
    )(me, mine, other, initial, demand)


def swap(x, m, size):
    return lax.ppermute(x, "gx", [(i, i ^ m) for i in range(size)])


def on_device(nx, ny, demand, initial):
    me = lax.axis_index("gx").astype(jnp.int32).reshape(1)
    fibres = lax.all_to_all(demand, "gx", 0, 1, tiled=True)[0]
    theirs = swap(gram_half(fibres, me, 1), 1, nx)
    half = gram_half(fibres, me, 0) + theirs
    rows, cols = half.shape
    share = lax.all_to_all(half.reshape(ny, rows // ny, cols), "gy", 0, 0, tiled=True)
    share = jnp.sum(share, 0)
    for m in (2, 4, 8):
        share = share + swap(share, m, nx)
    copies = jnp.broadcast_to(share[None], (ny,) + share.shape)
    half = lax.all_to_all(copies, "gy", 0, 0, tiled=True).reshape(rows, cols)
    basis, part = iterate(half, swap(half, 1, nx), initial, fibres, me)
    part = part.reshape(nx, part.shape[0] // nx, part.shape[1])
    core = lax.all_to_all(part, "gx", 0, 0, tiled=True)
    return (basis, jnp.transpose(core, (1, 0, 2)))


def solution(mesh):
    in_specs = (P(None, "gx", "gy"), P())
    out_specs = (P(), P("gx", None, "gy"))
    sizes = (mesh.shape["gx"], mesh.shape["gy"])
    return jax.shard_map(
        functools.partial(on_device, *sizes),
        mesh=mesh,
        in_specs=in_specs,
        out_specs=out_specs,
        check_vma=False,
    )
```
